32 devices in a mesh: surf: 8 (over z, x), col: 4 (over y, core).
Axes of the slice: x: 2, y: 2, z: 4, core: 2. Of those that a mesh axis runs over, the one named last changes fastest.
Arguments:
- stiffness: float32 [32, 3, 512, 512], P(('surf', 'col'))
- load: float32 [32, 3, 512, 256], P(('surf', 'col')), may hold values from -6 to 6
- start: float32 [32, 3, 512, 256], P(('surf', 'col')), may hold values from -6 to 6
- boundary_matrix: float32 [512, 4, 2048], P('surf', None, 'col'), may hold values from -0.125 to 0.125
- bem_node: int32 [4, 512], P('col'), may hold values from 0 to 511, as said below
Outputs:
- solution_field: float32 [32, 3, 512, 256], P(('surf', 'col'))
- traction: float32 [4, 512, 256], P('col', 'surf')
The draws below stay inside these ranges and needn't reach their ends.
Inputs may be any that keep to these rules, and one draw needn't show every extreme that they name: Each row bem_node[g] is a permutation of 0 to 512 - 1 (the top face nodes of column group g). For each block of 64 slots q in [s * 64, (s + 1) * 64) and each patch s2 of the group, the block's slots name either exactly 8 node of patch s2 or none; each patch's top face nodes lie in exactly 8 blocks.
All inputs are finite; a program needn't handle non-finite values.
Results may differ from the reference program's by a relative error of at most 0.0001.
Values sent between devices are 32-bit elements; how exact they have to be, the bound alone decides.
No kernel may reach another device: no remote copies, remote signals or barrier semaphores. Data moves between devices by JAX's collectives and lax.ppermute only.
A program may use at most 128 MiB of HBM per device.

```python
import jax
import jax.numpy as jnp
from jax import lax

EDGE = 8
DEPTH = 3
FIELDS = 256
ITERS = 2
EL_NODES = 512
N_PATCH = 32
CB = 512
NB = 2048
N_SURF = 8
N_COL = 4


def draw_stiffness(key, part):
    first = jax.random.fold_in(key, 0)
    shape = (N_PATCH, DEPTH, EL_NODES, EL_NODES)
    identity = jnp.eye(EL_NODES, dtype=jnp.float32)
    offdiag = jax.random.normal(first, shape, jnp.float32) * (0.6 / EL_NODES ** 0.5)
    return offdiag + 2.0 * identity


def draw_bem_node(key, part):
    face_nodes = EDGE * EDGE
    per_pair = max(face_nodes // N_SURF, 1)
    reach = min(N_SURF, face_nodes)

    def one_group(group_key):
        key_a, key_b, key_c, key_d = jax.random.split(group_key, 4)
        labels = jax.random.permutation(key_a, N_SURF)
        offsets = jax.random.permutation(key_b, N_SURF)
        slot_perm = jax.vmap(lambda small: jax.random.permutation(small, face_nodes))(jax.random.split(key_c, N_SURF))
        node_perm = jax.vmap(lambda small: jax.random.permutation(small, face_nodes))(jax.random.split(key_d, N_SURF))
        holder = jnp.arange(N_SURF, dtype=jnp.int32)[:, None]
        remain = slot_perm % reach
        within = slot_perm // reach
        owner = labels[(offsets[holder] + remain) % N_SURF]
        local_rank = remain * per_pair + within
        node_local = node_perm[owner, local_rank]
        return (owner * face_nodes + node_local).reshape(-1).astype(jnp.int32)
    return jax.vmap(one_group)(jax.random.split(key, N_COL))


def block_scale(rng, extent, shards, low, high):
    loudness, own = 1.0, jax.random.fold_in(rng, 6)
    for dim, blocks in shards:
        heights = jnp.exp(jax.random.uniform(jax.random.fold_in(own, dim), (blocks,), jnp.float32, low / len(shards), high / len(shards)))
        loudness = loudness * jnp.repeat(heights, extent[dim] // blocks).reshape([-1 if axis == dim else 1 for axis in range(len(extent))])
    return loudness


def scatter_about(rng, extent, deviation, bound, pieces=(), kind=jnp.bfloat16):
    gain = block_scale(rng, extent, pieces, -0.22, 0.18) if pieces else 1.0
    array = jax.random.normal(rng, extent, jnp.float32) * deviation * gain
    return jnp.minimum(jnp.maximum(array, -bound), bound).astype(kind)


def setup_inputs(seed: int = 0) -> dict:
    key_of = jax.random.split(jax.random.key(seed), 6)
    stiffness = draw_stiffness(jax.random.fold_in(key_of[5], 71), 0)
    load = scatter_about(key_of[1], (N_PATCH, DEPTH, EL_NODES, FIELDS), 1.0, 6.0, ((0, 32),), jnp.float32)
    start = scatter_about(key_of[2], (N_PATCH, DEPTH, EL_NODES, FIELDS), 1.0, 6.0, ((0, 32),), jnp.float32)
    boundary_matrix = scatter_about(key_of[3], (CB, N_COL, NB), NB ** -0.5, 0.125, ((0, 8), (2, 4)), jnp.float32)
    bem_node = draw_bem_node(jax.random.fold_in(key_of[5], 71), 0)
    return dict(stiffness=stiffness, load=load, start=start, boundary_matrix=boundary_matrix, bem_node=bem_node)


damping = 0.25
coupling = 0.5


def face_terms(cube):
    low_i = cube[:, :, :, 0]
    high_i = cube[:, :, :, -1]
    below = jnp.concatenate([jnp.zeros_like(high_i[:1]), high_i[:-1]], axis=0)
    above = jnp.concatenate([low_i[1:], jnp.zeros_like(low_i[:1])], axis=0)
    extra = jnp.zeros_like(cube)
    extra = extra.at[:, :, :, 0].add(low_i - below)
    extra = extra.at[:, :, :, -1].add(high_i - above)
    low_j = cube[:, :, :, :, 0]
    high_j = cube[:, :, :, :, -1]
    left_side = jnp.concatenate([jnp.zeros_like(high_j[:, :1]), high_j[:, :-1]], axis=1)
    right_side = jnp.concatenate([low_j[:, 1:], jnp.zeros_like(low_j[:, :1])], axis=1)
    extra = extra.at[:, :, :, :, 0].add(low_j - left_side)
    extra = extra.at[:, :, :, :, -1].add(high_j - right_side)
    low_k = cube[:, :, :, :, :, 0]
    high_k = cube[:, :, :, :, :, -1]
    deeper = jnp.concatenate([low_k[:, :, 1:], jnp.zeros_like(low_k[:, :, :1])], axis=2)
    extra = extra.at[:, :, :, :, :, -1].add(high_k - deeper)
    extra = extra.at[:, :, 1:, :, :, 0].add(low_k[:, :, 1:] - high_k[:, :, :-1])
    return extra


def reference(stiffness, load, start, boundary_matrix, bem_node):
    highest = lax.Precision.HIGHEST
    shape_seven = (N_SURF, N_COL, DEPTH, EDGE, EDGE, EDGE, FIELDS)
    shape_five = (N_SURF, N_COL, DEPTH, EL_NODES, FIELDS)
    stiff_five = stiffness.reshape(N_SURF, N_COL, DEPTH, EL_NODES, EL_NODES)
    load_seven = load.reshape(shape_seven)
    current = start.reshape(shape_five)
    inverse = jnp.argsort(bem_node, axis=1).astype(jnp.int32)
    operator_rows = boundary_matrix.reshape(CB * N_COL, NB)
    traction = jnp.zeros((N_COL, CB, FIELDS), jnp.float32)
    for turn_index in range(ITERS):
        cube = current.reshape(shape_seven)
        top_face = cube[:, :, 0, :, :, 0, :]
        by_group = jnp.transpose(top_face, (1, 0, 2, 3, 4)).reshape(N_COL, CB, FIELDS)
        trace = jnp.take_along_axis(by_group, bem_node[:, :, None], axis=1)
        flat = jnp.dot(operator_rows, trace.reshape(NB, FIELDS), precision=highest,
                       preferred_element_type=jnp.float32)
        traction = jnp.transpose(flat.reshape(CB, N_COL, FIELDS), (1, 0, 2))
        on_nodes = jnp.take_along_axis(traction, inverse[:, :, None], axis=1)
        on_nodes = jnp.transpose(on_nodes.reshape(N_COL, N_SURF, EDGE, EDGE, FIELDS), (1, 0, 2, 3, 4))
        applied = jnp.einsum('scdab,scdbf->scdaf', stiff_five, current, precision=highest)
        applied = applied.reshape(shape_seven) + coupling * face_terms(cube)
        applied = applied.at[:, :, 0, :, :, 0, :].add(on_nodes)
        residual = load_seven - applied
        current = (cube + damping * residual).reshape(shape_five)
    return current.reshape(N_PATCH, DEPTH, EL_NODES, FIELDS), traction
```

```python
import functools

import jax
import jax.numpy as jnp
from jax import lax
from jax.experimental import pallas as pl
from jax.experimental.pallas import tpu as pltpu
from jax.sharding import PartitionSpec as P

EDGE = 8
FACE = EDGE * EDGE
NODES = EDGE * FACE
damping = 0.25
coupling = 0.5
HIGH = lax.Precision.HIGHEST
F32 = jnp.float32
BF16 = jnp.bfloat16
VMEM = pl.BlockSpec(memory_space=pltpu.VMEM)


def peer(index, step, count):
    if count & (count - 1) == 0:
        return index ^ step
    return (index + step) % count


def split(x):
    high = x.astype(BF16)
    return high, (x - high.astype(F32)).astype(BF16)


def dot(a, b):
    return jnp.dot(a, b, preferred_element_type=F32)


def dot_nt(a, b):
    return lax.dot_general(a, b, (((1,), (1,)), ((), ())), preferred_element_type=F32)


def dot_three(a_high, a_low, b):
    b_high, b_low = split(b)
    return dot(a_high, b_high) + (dot(a_high, b_low) + dot(a_low, b_high))


def dot_exact(a, b):
    return jnp.dot(a, b, preferred_element_type=F32, precision=HIGH)


def struct(shape, dtype=F32):
    return jax.ShapeDtypeStruct(shape, dtype)


def cost(flops, nbytes):
    return pl.CostEstimate(flops=flops, bytes_accessed=nbytes, transcendentals=0)


def write_faces(layers, u, a_i, b_i, a_j, b_j):
    odd_s = lax.rem(lax.axis_index("surf"), 2)
    odd_c = lax.rem(lax.axis_index("col"), 2)
    rows_a = pl.multiple_of((1 - odd_s) * (NODES - FACE), FACE)
    rows_b = pl.multiple_of(odd_s * (NODES - FACE), FACE)
    j_a = (1 - odd_c) * (FACE - EDGE)
    j_b = odd_c * (FACE - EDGE)
    for d in range(layers):
        a_i[d] = u[d, pl.ds(rows_a, FACE), :]
        b_i[d] = u[d, pl.ds(rows_b, FACE), :]
        for i in range(EDGE):
            to = pl.ds(i * EDGE, EDGE)
            a_j[d, to, :] = u[d, pl.ds(pl.multiple_of(i * FACE + j_a, EDGE), EDGE), :]
            b_j[d, to, :] = u[d, pl.ds(pl.multiple_of(i * FACE + j_b, EDGE), EDGE), :]


def layer_of(value, k):
    return value.reshape(FACE, EDGE, value.shape[-1])[:, k, :]


def put_layer(base, value, k):
    fields = base.shape[-1]
    height = lax.broadcasted_iota(jnp.int32, (FACE, EDGE, fields), 1)
    wide = jnp.broadcast_to(value[:, None, :], (FACE, EDGE, fields))
    return base + jnp.where(height == k, wide, 0.0).reshape(NODES, fields)


def extract_kernel(layers, copies, u, top, a_i, b_i, a_j, b_j):
    value = layer_of(u[0], 0)
    for p in range(copies):
        top[p] = value
    write_faces(layers, u, a_i, b_i, a_j, b_j)


def extract(u, copies):
    layers, _, fields = u.shape
    face = struct((layers, FACE, fields))
    return pl.pallas_call(
        functools.partial(extract_kernel, layers, copies),
        out_shape=[struct((copies, FACE, fields))] + [face] * 4,
        in_specs=[VMEM],
        out_specs=[VMEM] * 5,
        name="extract",
    )(u)


def update_kernel(layers, v, top, u, a_i, b_i, a_j, b_j):
    u[...] = v[...]
    base = v[0]
    u[0] = put_layer(base, top[...] - layer_of(base, 0), 0)
    write_faces(layers, u, a_i, b_i, a_j, b_j)


def update(v, top):
    layers, _, fields = v.shape
    face = struct((layers, FACE, fields))
    return pl.pallas_call(
        functools.partial(update_kernel, layers),
        out_shape=[struct(v.shape)] + [face] * 4,
        in_specs=[VMEM] * 2,
        out_specs=[VMEM] * 5,
        name="update",
    )(v, top)


def swap_faces(faces):
    out = []
    for axis, (first, second) in zip(("surf", "col"), (faces[:2], faces[2:])):
        count = lax.axis_size(axis)
        pairs_a = [(i, i ^ 1) for i in range(count) if i ^ 1 < count]
        pairs_b = [(i, ((i + 1) ^ 1) - 1) for i in range(1, count) if ((i + 1) ^ 1) - 1 < count]
        out.append(lax.ppermute(first, axis, pairs_a))
        out.append(lax.ppermute(second, axis, pairs_b))
    return out


def tables_kernel(cols, per_pair, block, bem, m, m1h, m1l, m2h, m2l, own, x, xt, y, yt, ah, al):
    group = bem.shape[1]
    s = lax.axis_index("surf")
    c = lax.axis_index("col")
    step = pl.program_id(0)
    nodes = bem[...]

    @pl.when(step == 0)
    def _():
        for k in range(cols):
            high, low = split(m[peer(c, k, cols)])
            ah[pl.ds(k * FACE, FACE), :] = high
            al[pl.ds(k * FACE, FACE), :] = low
        lane = lax.broadcasted_iota(jnp.int32, (FACE, group), 1)
        mine = lax.broadcasted_iota(jnp.int32, (FACE, group), 0) + s * FACE
        nodes_all = jnp.broadcast_to(nodes, (FACE, group))
        r = lax.broadcasted_iota(jnp.int32, (FACE, FACE), 0)
        l = lax.broadcasted_iota(jnp.int32, (FACE, FACE), 1)

        def column(mask, value):
            return jnp.sum(jnp.where(mask, value, 0.0), axis=1, keepdims=True)

        def row(mask, value):
            return dot_nt(value.astype(BF16), jnp.where(mask, 1.0, 0.0).astype(BF16))

        hit = nodes_all == mine
        own[...] = jnp.where(hit, 1.0, 0.0).astype(BF16)
        block_of = (lane // FACE).astype(F32)
        hold_c, hold_r = column(hit, block_of), row(hit, block_of)
        same = hold_c == hold_r
        rank_r = jnp.sum(jnp.where(same & (r < l), 1.0, 0.0), axis=0, keepdims=True)
        rank_c = jnp.sum(jnp.where(same & (l < r), 1.0, 0.0), axis=1, keepdims=True)
        place_r = (hold_r * per_pair + rank_r).astype(jnp.int32)
        place_c = (hold_c * per_pair + rank_c).astype(jnp.int32)
        x[...] = jnp.where(r == place_r, 1.0, 0.0)
        xt[...] = jnp.where(l == place_c, 1.0, 0.0)

        hit = lane == mine
        owner = (nodes_all // FACE).astype(F32)
        local = lax.rem(nodes_all, FACE).astype(F32)
        own_c, own_r = column(hit, owner), row(hit, owner)
        loc_c, loc_r = column(hit, local), row(hit, local)
        same = own_c == own_r
        rank_r = jnp.sum(jnp.where(same & (loc_c < loc_r), 1.0, 0.0), axis=0, keepdims=True)
        rank_c = jnp.sum(jnp.where(same & (loc_r < loc_c), 1.0, 0.0), axis=1, keepdims=True)
        place_r = (own_r * per_pair + rank_r).astype(jnp.int32)
        place_c = (own_c * per_pair + rank_c).astype(jnp.int32)
        y[...] = jnp.where(l == place_c, 1.0, 0.0)
        yt[...] = jnp.where(r == place_r, 1.0, 0.0)

    here = pl.ds(pl.multiple_of(step * block, block), block)
    m2h[...] = ah[:, here]
    m2l[...] = al[:, here]
    node = lax.broadcasted_iota(jnp.int32, (block, group), 0) + step * block
    pick = jnp.where(nodes == node, 1.0, 0.0).astype(BF16)
    m1h[...] = dot_nt(ah[...], pick).astype(BF16)
    m1l[...] = dot_nt(al[...], pick).astype(BF16)


def tables(bem, m, per_pair):
    cols, _, group = m.shape
    rows = cols * FACE
    block = min(NODES, group)
    fixed = lambda shape: pl.BlockSpec(shape, lambda i: (0,) * len(shape))
    wide = pl.BlockSpec((rows, block), lambda i: (0, i))
    small = [struct((FACE, FACE))] * 4
    return pl.pallas_call(
        functools.partial(tables_kernel, cols, per_pair, block),
        grid=(group // block,),
        out_shape=[struct((rows, group), BF16)] * 4 + [struct((FACE, group), BF16)] + small,
        in_specs=[fixed((1, group)), fixed(m.shape)],
        out_specs=[wide] * 4 + [fixed((FACE, group))] + [fixed((FACE, FACE))] * 4,
        scratch_shapes=[pltpu.VMEM((rows, group), BF16)] * 2,
        cost_estimate=cost(4 * rows * group * group, 10 * rows * group),
        name="tables",
    )(bem, m)


def operator_kernel(cols, select, mh, ml, trace, *rest):
    if select:
        own, *outs = rest
    else:
        outs = rest
    value = trace[...]
    high, low = split(value)
    part = dot(mh[...], high) + (dot(mh[...], low) + dot(ml[...], high))
    for k in range(cols):
        outs[k][...] = part[k * FACE : (k + 1) * FACE]
    if select:
        rest_low = (value - high.astype(F32) - low.astype(F32)).astype(BF16)
        pick = own[...]
        outs[cols][...] = dot(pick, high) + (dot(pick, low) + dot(pick, rest_low))


def operator(cols, mh, ml, trace, own=None):
    group, fields = trace.shape
    block = struct((FACE, fields))
    select = own is not None
    outs = cols + select
    args = (mh, ml, trace) + ((own,) if select else ())
    return pl.pallas_call(
        functools.partial(operator_kernel, cols, select),
        out_shape=[block] * outs,
        in_specs=[VMEM] * len(args),
        out_specs=[VMEM] * outs,
        cost_estimate=cost(6 * cols * FACE * group * fields, 4 * group * fields),
        name="operator",
    )(*args)


def reduce_rows(parts):
    count = len(parts)
    got = [
        lax.ppermute(parts[k], "col", [(i, peer(i, k, count)) for i in range(count)])
        for k in range(1, count)
    ]
    return [parts[0]] + got


def next_trace_kernel(count, copies, *refs):
    parts, (y, sorted_v, out) = refs[:count], refs[count:]
    total = sum(p[...] for p in parts[1:]) + parts[0][...]
    value = dot_exact(y[...], sorted_v[...]) - damping * total
    for p in range(copies):
        out[p] = value


def next_trace(parts, y, sorted_v, copies):
    return pl.pallas_call(
        functools.partial(next_trace_kernel, len(parts), copies),
        out_shape=struct((copies,) + sorted_v.shape),
        in_specs=[VMEM] * (len(parts) + 2),
        out_specs=VMEM,
        name="next_trace",
    )(*parts, y, sorted_v)


def last_traction_kernel(count, *refs):
    parts, (yt, total_ref, sorted_ref) = refs[:count], refs[count:]
    total = sum(p[...] for p in parts[1:]) + parts[0][...]
    total_ref[...] = total
    sorted_ref[...] = dot_exact(yt[...], total)


def last_traction(parts, yt):
    return pl.pallas_call(
        functools.partial(last_traction_kernel, len(parts)),
        out_shape=[struct(parts[0].shape)] * 2,
        in_specs=[VMEM] * (len(parts) + 1),
        out_specs=[VMEM] * 2,
        name="last_traction",
    )(*parts, yt)


def volume_kernel(layers, sort, k, load, u, a_i, b_i, a_j, b_j, *rest):
    if sort:
        x, out, sorted_ref = rest
    else:
        (out,) = rest
    d = pl.program_id(0)
    odd_s = lax.rem(lax.axis_index("surf"), 2) == 1
    odd_c = lax.rem(lax.axis_index("col"), 2) == 1
    here = u[d]
    k_high, k_low = split(k[0])
    applied = dot_three(k_high, k_low, here)
    half = damping * coupling
    fields = here.shape[-1]
    height = lax.rem(lax.broadcasted_iota(jnp.int32, (NODES, fields), 0), EDGE)
    deeper = pltpu.roll(u[jnp.minimum(d + 1, layers - 1)], EDGE - 1, 0)
    deeper = here - jnp.where(d + 1 < layers, deeper, 0.0)
    above = here - pltpu.roll(u[jnp.maximum(d - 1, 0)], NODES - EDGE + 1, 0)
    above = jnp.where(d > 0, above, 0.0)
    vertical = jnp.where(height == EDGE - 1, deeper, jnp.where(height == 0, above, 0.0))
    out[0] = here + damping * (load[0] - applied) - half * vertical

    def face(rows, value):
        out[0, rows, :] = out[0, rows, :] - half * (u[d, rows, :] - value)

    low, high = pl.ds(0, FACE), pl.ds(NODES - FACE, FACE)
    got_a, got_b = a_i[d], b_i[d]
    face(low, jnp.where(odd_s, got_a, got_b))
    face(high, jnp.where(odd_s, got_b, got_a))
    for i in range(EDGE):
        rows = pl.ds(i * EDGE, EDGE)
        got_a, got_b = a_j[d, rows, :], b_j[d, rows, :]
        face(pl.ds(i * FACE, EDGE), jnp.where(odd_c, got_a, got_b))
        face(pl.ds(i * FACE + FACE - EDGE, EDGE), jnp.where(odd_c, got_b, got_a))
    if sort:
        @pl.when(d == 0)
        def _():
            sorted_ref[...] = dot_exact(x[...], layer_of(out[0], 0))


def volume(kmats, load, u, faces, x=None):
    layers, nodes, fields = u.shape
    sort = x is not None
    whole = lambda a: pl.BlockSpec(a.shape, lambda d: (0,) * a.ndim)
    layer = pl.BlockSpec((1, nodes, fields), lambda d: (d, 0, 0))
    args = (kmats, load, u, *faces) + ((x,) if sort else ())
    shapes, specs = [struct(u.shape)], [layer]
    if sort:
        shapes.append(struct((FACE, fields)))
        specs.append(pl.BlockSpec((FACE, fields), lambda d: (0, 0)))
    return pl.pallas_call(
        functools.partial(volume_kernel, layers, sort),
        grid=(layers,),
        out_shape=shapes,
        in_specs=[pl.BlockSpec((1, nodes, nodes), lambda d: (d, 0, 0)), layer]
        + [whole(a) for a in args[2:]],
        out_specs=specs,
        cost_estimate=cost(6 * layers * nodes * nodes * fields, 4 * layers * nodes * (nodes + 3 * fields)),
        name="volume",
    )(*args)


def finish_kernel(w, xt, got, out):
    out[0] = put_layer(w[0], -damping * dot_exact(xt[...], got[...]), 0)


def finish(w, xt, got):
    _, nodes, fields = w.shape
    layer = pl.BlockSpec((1, nodes, fields), lambda i: (0, 0, 0))
    whole = lambda a: pl.BlockSpec(a.shape, lambda i: (0,) * a.ndim)
    return pl.pallas_call(
        finish_kernel,
        grid=(1,),
        out_shape=struct(w.shape),
        in_specs=[layer, whole(xt), whole(got)],
        out_specs=layer,
        input_output_aliases={0: 0},
        name="finish",
    )(w, xt, got)


def exchange(blocks):
    return lax.all_to_all(blocks, "surf", split_axis=0, concat_axis=0, tiled=True)


def shards(stiffness, load, start, boundary_matrix, bem_node):
    surfs, cols = lax.axis_size("surf"), lax.axis_size("col")
    per_pair = max(FACE // surfs, 1)
    kmats, load, u = stiffness[0], load[0], start[0]
    fields = load.shape[2]
    flat = (surfs * FACE, fields)

    top, *faces = extract(u, surfs)
    gathered = exchange(top).reshape(flat)
    m1h, m1l, m2h, m2l, own, x, xt, y, yt = tables(
        bem_node, jnp.transpose(boundary_matrix, (1, 0, 2)), per_pair
    )
    v, sorted_v = volume(kmats, load, u, swap_faces(faces), x)
    sorted_v = exchange(sorted_v.reshape(surfs, per_pair, fields)).reshape(FACE, fields)
    parts = reduce_rows(operator(cols, m1h, m1l, gathered))
    gathered = exchange(next_trace(parts, y, sorted_v, surfs)).reshape(flat)
    *parts, top = operator(cols, m2h, m2l, gathered, own)
    parts = reduce_rows(parts)
    u, *faces = update(v, top)
    (w,) = volume(kmats, load, u, swap_faces(faces))
    traction, back = last_traction(parts, yt)
    back = exchange(back.reshape(surfs, per_pair, fields)).reshape(FACE, fields)
    return finish(w, xt, back)[None], traction[None]


def solution(mesh):
    cell = P(("surf", "col"), None, None, None)
    return jax.shard_map(
        shards,
        mesh=mesh,
        in_specs=(cell, cell, cell, P("surf", None, "col"), P("col", None)),
        out_specs=(cell, P("col", "surf", None)),
        check_vma=False,
    )
```

```python
import functools

import jax
import jax.numpy as jnp
from jax import lax
from jax.experimental import pallas as pl
from jax.experimental.pallas import tpu as pltpu
from jax.sharding import PartitionSpec as P

EDGE = 8
FACE = EDGE * EDGE
NODES = EDGE * FACE
damping = 0.25
coupling = 0.5
MAX_PERMUTES = 16
HIGH = lax.Precision.HIGHEST
F32 = jnp.float32
BF16 = jnp.bfloat16
VMEM = pl.BlockSpec(memory_space=pltpu.VMEM)


def peer(index, step, count):
    if count & (count - 1) == 0:
        return index ^ step
    return (index + step) % count


def split(x):
    high = x.astype(BF16)
    return high, (x - high.astype(F32)).astype(BF16)


def dot(a, b):
    return jnp.dot(a, b, preferred_element_type=F32)


def dot_nt(a, b):
    return lax.dot_general(a, b, (((1,), (1,)), ((), ())), preferred_element_type=F32)


def dot_three(a_high, a_low, b):
    b_high, b_low = split(b)
    return dot(a_high, b_high) + (dot(a_high, b_low) + dot(a_low, b_high))


def dot_exact(a, b):
    return jnp.dot(a, b, preferred_element_type=F32, precision=HIGH)


def struct(shape, dtype=F32):
    return jax.ShapeDtypeStruct(shape, dtype)


def cost(flops, nbytes):
    return pl.CostEstimate(flops=flops, bytes_accessed=nbytes, transcendentals=0)


def write_faces(layers, u, a_i, b_i, a_j, b_j):
    odd_s = lax.rem(lax.axis_index("surf"), 2)
    odd_c = lax.rem(lax.axis_index("col"), 2)
    rows_a = pl.multiple_of((1 - odd_s) * (NODES - FACE), FACE)
    rows_b = pl.multiple_of(odd_s * (NODES - FACE), FACE)
    j_a = (1 - odd_c) * (FACE - EDGE)
    j_b = odd_c * (FACE - EDGE)
    for d in range(layers):
        a_i[d] = u[d, pl.ds(rows_a, FACE), :]
        b_i[d] = u[d, pl.ds(rows_b, FACE), :]
        for i in range(EDGE):
            to = pl.ds(i * EDGE, EDGE)
            a_j[d, to, :] = u[d, pl.ds(pl.multiple_of(i * FACE + j_a, EDGE), EDGE), :]
            b_j[d, to, :] = u[d, pl.ds(pl.multiple_of(i * FACE + j_b, EDGE), EDGE), :]


def layer_of(value, k):
    return value.reshape(FACE, EDGE, value.shape[-1])[:, k, :]


def put_layer(base, value, k):
    fields = base.shape[-1]
    height = lax.broadcasted_iota(jnp.int32, (FACE, EDGE, fields), 1)
    wide = jnp.broadcast_to(value[:, None, :], (FACE, EDGE, fields))
    return base + jnp.where(height == k, wide, 0.0).reshape(NODES, fields)


def top_kernel(copies, u, top):
    value = layer_of(u[0], 0)
    for p in range(copies):
        top[p] = value


def top_copies(u, copies):
    _, nodes, fields = u.shape
    return pl.pallas_call(
        functools.partial(top_kernel, copies),
        grid=(1,),
        out_shape=struct((copies, FACE, fields)),
        in_specs=[pl.BlockSpec((1, nodes, fields), lambda i: (0, 0, 0))],
        out_specs=VMEM,
        name="top_copies",
    )(u)


def faces_of(u):
    layers, _, fields = u.shape
    return pl.pallas_call(
        functools.partial(write_faces, layers),
        out_shape=[struct((layers, FACE, fields))] * 4,
        in_specs=[VMEM],
        out_specs=[VMEM] * 4,
        name="faces_of",
    )(u)


def update_kernel(layers, v, top, u, a_i, b_i, a_j, b_j):
    u[...] = v[...]
    base = v[0]
    u[0] = put_layer(base, top[...] - layer_of(base, 0), 0)
    write_faces(layers, u, a_i, b_i, a_j, b_j)


def update(v, top):
    layers, _, fields = v.shape
    face = struct((layers, FACE, fields))
    return pl.pallas_call(
        functools.partial(update_kernel, layers),
        out_shape=[struct(v.shape)] + [face] * 4,
        in_specs=[VMEM] * 2,
        out_specs=[VMEM] * 5,
        name="update",
    )(v, top)


def swap_faces(faces):
    out = []
    for axis, (first, second) in zip(("surf", "col"), (faces[:2], faces[2:])):
        count = lax.axis_size(axis)
        pairs_a = [(i, i ^ 1) for i in range(count) if i ^ 1 < count]
        pairs_b = [(i, ((i + 1) ^ 1) - 1) for i in range(1, count) if ((i + 1) ^ 1) - 1 < count]
        out.append(lax.ppermute(first, axis, pairs_a))
        out.append(lax.ppermute(second, axis, pairs_b))
    return out


def tables_kernel(cols, per_pair, count, bem, m, nh, nl, ch, cl, own, xt, yt, ah, al):
    group = bem.shape[1]
    s = lax.axis_index("surf")
    c = lax.axis_index("col")
    step = pl.program_id(0)
    nodes_all = jnp.broadcast_to(bem[...], (FACE, group))
    lane = lax.broadcasted_iota(jnp.int32, (FACE, group), 1)
    index = lax.broadcasted_iota(jnp.int32, (FACE, group), 0)
    mine = index + s * FACE
    hit_node = nodes_all == mine

    @pl.when(step == 0)
    def _():
        for k in range(cols):
            high, low = split(m[peer(c, k, cols)])
            ah[pl.ds(k * FACE, FACE), :] = high
            al[pl.ds(k * FACE, FACE), :] = low
        r = lax.broadcasted_iota(jnp.int32, (FACE, FACE), 0)
        l = lax.broadcasted_iota(jnp.int32, (FACE, FACE), 1)

        def column(mask, value):
            return jnp.sum(jnp.where(mask, value, 0.0), axis=1, keepdims=True)

        def row(mask, value):
            return dot_nt(value.astype(BF16), jnp.where(mask, 1.0, 0.0).astype(BF16))

        block_of = (lane // FACE).astype(F32)
        hold_c, hold_r = column(hit_node, block_of), row(hit_node, block_of)
        same = (hold_c == hold_r) & (l < r)
        rank_c = jnp.sum(jnp.where(same, 1.0, 0.0), axis=1, keepdims=True)
        place_c = (hold_c * per_pair + rank_c).astype(jnp.int32)
        xt[...] = jnp.where(l == place_c, 1.0, 0.0)

        hit = lane == mine
        owner = (nodes_all // FACE).astype(F32)
        local = lax.rem(nodes_all, FACE).astype(F32)
        own_c, own_r = column(hit, owner), row(hit, owner)
        loc_c, loc_r = column(hit, local), row(hit, local)
        same = (own_c == own_r) & (loc_c < loc_r)
        rank_r = jnp.sum(jnp.where(same, 1.0, 0.0), axis=0, keepdims=True)
        place_r = (own_r * per_pair + rank_r).astype(jnp.int32)
        yt[...] = jnp.where(r == place_r, 1.0, 0.0)

    ones_own = jnp.where(hit_node, 1.0, 0.0).astype(BF16)
    high, low = ah[...], al[...]
    for q in range(count):
        block = (s ^ (step * count + q)) * FACE
        by_slot = jnp.where(lane == index + block, -damping, 0.0).astype(BF16)
        by_node = jnp.where(nodes_all == index + block, 1.0, 0.0).astype(BF16)
        pick = jnp.concatenate([by_slot, by_node], axis=0)
        here = pl.ds(q * 2 * FACE, 2 * FACE)
        picked_high = dot_nt(high, pick).astype(BF16)
        picked_low = dot_nt(low, pick).astype(BF16)
        ch[:, here] = picked_high
        cl[:, here] = picked_low
        nh[:, pl.ds(q * FACE, FACE)] = picked_high[:, FACE:]
        nl[:, pl.ds(q * FACE, FACE)] = picked_low[:, FACE:]
        own[:, here] = dot_nt(ones_own, pick).astype(BF16)


def tables(bem, m, per_pair):
    cols, _, group = m.shape
    rows = cols * FACE
    surfs = group // FACE
    count = min(surfs, EDGE)
    fixed = lambda shape: pl.BlockSpec(shape, lambda i: (0,) * len(shape))
    wide = lambda height, width: pl.BlockSpec((height, width), lambda i: (0, i))
    return pl.pallas_call(
        functools.partial(tables_kernel, cols, per_pair, count),
        grid=(surfs // count,),
        out_shape=[struct((rows, group), BF16)] * 2
        + [struct((rows, 2 * group), BF16)] * 2
        + [struct((FACE, 2 * group), BF16)]
        + [struct((FACE, FACE))] * 2,
        in_specs=[fixed((1, group)), fixed(m.shape)],
        out_specs=[wide(rows, count * FACE)] * 2
        + [wide(rows, 2 * count * FACE)] * 2
        + [wide(FACE, 2 * count * FACE)]
        + [fixed((FACE, FACE))] * 2,
        scratch_shapes=[pltpu.VMEM((rows, group), BF16)] * 2,
        cost_estimate=cost(8 * rows * group * group, 10 * rows * group),
        name="tables",
    )(bem, m)


def operator_kernel(cols, blocks, select, mh, ml, *refs):
    s = lax.axis_index("surf")
    if select:
        own, *refs = refs
    if len(blocks) == 1:
        trace = [refs[0][s ^ p] for p in range(blocks[0])]
    else:
        trace = [ref[...] for ref in refs[: len(blocks)]]
    outs = refs[len(blocks) :]
    value = jnp.concatenate(trace, axis=0)
    high, low = split(value)
    part = dot(mh[...], high) + (dot(mh[...], low) + dot(ml[...], high))
    for k in range(cols):
        outs[k][...] = part[k * FACE : (k + 1) * FACE]
    if select:
        rest = (value - high.astype(F32) - low.astype(F32)).astype(BF16)
        pick = own[...]
        outs[cols][...] = dot(pick, high) + (dot(pick, low) + dot(pick, rest))


def operator(cols, mh, ml, trace, own=None):
    trace = trace if isinstance(trace, list) else [trace]
    fields = trace[0].shape[-1]
    block = struct((FACE, fields))
    select = own is not None
    outs = cols + select
    args = (mh, ml) + ((own,) if select else ()) + tuple(trace)
    return pl.pallas_call(
        functools.partial(operator_kernel, cols, [t.shape[0] for t in trace], select),
        out_shape=[block] * outs,
        in_specs=[VMEM] * len(args),
        out_specs=[VMEM] * outs,
        cost_estimate=cost(6 * mh.size * fields, 4 * mh.size + 4 * mh.shape[1] * fields),
        name="operator",
    )(*args)


def gather_blocks(x, axis):
    count = lax.axis_size(axis)
    if count & (count - 1) or count > MAX_PERMUTES:
        return exchange(jnp.broadcast_to(x[None], (count,) + x.shape))

    def send(block, step):
        return lax.ppermute(block, axis, [(i, i ^ step) for i in range(count)])

    half = count // 2
    far = send(x, half)
    steps = [*range(2, half), 1]
    near = {step: send(x, step) for step in steps}
    passed = {step + half: send(far, step) for step in steps}
    found = {0: x, half: far, **near, **passed}
    return [found[step] for step in range(count)]


def reduce_rows(parts):
    count = len(parts)
    got = [
        lax.ppermute(parts[k], "col", [(i, peer(i, k, count)) for i in range(count)])
        for k in range(1, count)
    ]
    return [parts[0]] + got


def traction_kernel(count, *refs):
    parts, (top, out) = refs[:count], refs[count:]
    out[pl.ds(0, FACE), :] = sum(p[...] for p in parts[1:]) + parts[0][...]
    out[pl.ds(FACE, FACE), :] = top[...]


def traction_and_top(parts, top):
    return pl.pallas_call(
        functools.partial(traction_kernel, len(parts)),
        out_shape=struct((2 * FACE, top.shape[1])),
        in_specs=[VMEM] * (len(parts) + 1),
        out_specs=VMEM,
        name="traction_and_top",
    )(*parts, top)


def last_traction_kernel(count, *refs):
    parts, (yt, total_ref, sorted_ref) = refs[:count], refs[count:]
    total = sum(p[...] for p in parts[1:]) + parts[0][...]
    total_ref[...] = total
    sorted_ref[...] = dot_exact(yt[...], total)


def last_traction(parts, yt):
    return pl.pallas_call(
        functools.partial(last_traction_kernel, len(parts)),
        out_shape=[struct(parts[0].shape)] * 2,
        in_specs=[VMEM] * (len(parts) + 1),
        out_specs=[VMEM] * 2,
        name="last_traction",
    )(*parts, yt)


def volume_kernel(layers, k, load, u, out):
    d = pl.program_id(0)
    here = u[d]
    k_high, k_low = split(k[0])
    applied = dot_three(k_high, k_low, here)
    half = damping * coupling
    fields = here.shape[-1]
    height = lax.rem(lax.broadcasted_iota(jnp.int32, (NODES, fields), 0), EDGE)
    deeper = pltpu.roll(u[jnp.minimum(d + 1, layers - 1)], EDGE - 1, 0)
    deeper = here - jnp.where(d + 1 < layers, deeper, 0.0)
    above = here - pltpu.roll(u[jnp.maximum(d - 1, 0)], NODES - EDGE + 1, 0)
    above = jnp.where(d > 0, above, 0.0)
    vertical = jnp.where(height == EDGE - 1, deeper, jnp.where(height == 0, above, 0.0))
    out[0] = here + damping * (load[0] - applied) - half * vertical

    def own_face(rows):
        out[0, rows, :] = out[0, rows, :] - half * u[d, rows, :]

    own_face(pl.ds(0, FACE))
    own_face(pl.ds(NODES - FACE, FACE))
    for i in range(EDGE):
        own_face(pl.ds(i * FACE, EDGE))
        own_face(pl.ds(i * FACE + FACE - EDGE, EDGE))


def volume(kmats, load, u):
    layers, nodes, fields = u.shape
    layer = pl.BlockSpec((1, nodes, fields), lambda d: (d, 0, 0))
    return pl.pallas_call(
        functools.partial(volume_kernel, layers),
        grid=(layers,),
        out_shape=struct(u.shape),
        in_specs=[
            pl.BlockSpec((1, nodes, nodes), lambda d: (d, 0, 0)),
            layer,
            pl.BlockSpec(u.shape, lambda d: (0, 0, 0)),
        ],
        out_specs=layer,
        cost_estimate=cost(6 * layers * nodes * nodes * fields, 4 * layers * nodes * (nodes + 3 * fields)),
        name="volume",
    )(kmats, load, u)


def add_neighbours(layers, out, a_i, b_i, a_j, b_j):
    odd_s = lax.rem(lax.axis_index("surf"), 2) == 1
    odd_c = lax.rem(lax.axis_index("col"), 2) == 1
    half = damping * coupling

    def face(d, rows, first, second, odd):
        out[d, rows, :] = out[d, rows, :] + half * jnp.where(odd, first, second)

    for d in range(layers):
        got_a, got_b = a_i[d], b_i[d]
        face(d, pl.ds(0, FACE), got_a, got_b, odd_s)
        face(d, pl.ds(NODES - FACE, FACE), got_b, got_a, odd_s)
        for i in range(EDGE):
            rows = pl.ds(i * EDGE, EDGE)
            got_a, got_b = a_j[d, rows, :], b_j[d, rows, :]
            face(d, pl.ds(i * FACE, EDGE), got_a, got_b, odd_c)
            face(d, pl.ds(i * FACE + FACE - EDGE, EDGE), got_b, got_a, odd_c)


def neighbours_kernel(layers, w, a_i, b_i, a_j, b_j, out, top):
    out[...] = w[...]
    add_neighbours(layers, out, a_i, b_i, a_j, b_j)
    top[...] = layer_of(out[0], 0)


def neighbours(w, faces):
    layers, _, fields = w.shape
    return pl.pallas_call(
        functools.partial(neighbours_kernel, layers),
        out_shape=[struct(w.shape), struct((FACE, fields))],
        in_specs=[VMEM] * 5,
        out_specs=[VMEM] * 2,
        name="neighbours",
    )(w, *faces)


def finish_kernel(layers, w, a_i, b_i, a_j, b_j, xt, got, out):
    out[...] = w[...]
    add_neighbours(layers, out, a_i, b_i, a_j, b_j)
    out[0] = put_layer(out[0], -damping * dot_exact(xt[...], got[...]), 0)


def finish(w, faces, xt, got):
    return pl.pallas_call(
        functools.partial(finish_kernel, w.shape[0]),
        out_shape=struct(w.shape),
        in_specs=[VMEM] * 7,
        out_specs=VMEM,
        name="finish",
    )(w, *faces, xt, got)


def exchange(blocks):
    return lax.all_to_all(blocks, "surf", split_axis=0, concat_axis=0, tiled=True)


def shards(stiffness, load, start, boundary_matrix, bem_node):
    surfs, cols = lax.axis_size("surf"), lax.axis_size("col")
    per_pair = max(FACE // surfs, 1)
    kmats, load, u = stiffness[0], load[0], start[0]
    fields = load.shape[2]
    gathered = exchange(top_copies(u, surfs))
    faces = swap_faces(faces_of(u))
    nh, nl, ch, cl, own, xt, yt = tables(
        bem_node, jnp.transpose(boundary_matrix, (1, 0, 2)), per_pair
    )
    v, top = neighbours(volume(kmats, load, u), faces)
    parts = reduce_rows(operator(cols, nh, nl, gathered))
    gathered = gather_blocks(traction_and_top(parts, top), "surf")
    *parts, top = operator(cols, ch, cl, gathered, own)
    parts = reduce_rows(parts)
    u, *faces = update(v, top)
    faces = swap_faces(faces)
    w = volume(kmats, load, u)
    traction, back = last_traction(parts, yt)
    back = exchange(back.reshape(surfs, per_pair, fields)).reshape(FACE, fields)
    return finish(w, faces, xt, back)[None], traction[None]


def solution(mesh):
    cell = P(("surf", "col"), None, None, None)
    return jax.shard_map(
        shards,
        mesh=mesh,
        in_specs=(cell, cell, cell, P("surf", None, "col"), P("col", None)),
        out_specs=(cell, P("col", "surf", None)),
        check_vma=False,
    )
```

```python
import functools

import jax
import jax.numpy as jnp
from jax import lax
from jax.experimental import pallas as pl
from jax.experimental.pallas import tpu as pltpu
from jax.sharding import PartitionSpec as P

EDGE = 8
FACE = EDGE * EDGE
NODES = EDGE * FACE
damping = 0.25
coupling = 0.5
MAX_PERMUTES = 16
HIGH = lax.Precision.HIGHEST
F32 = jnp.float32
BF16 = jnp.bfloat16
VMEM = pl.BlockSpec(memory_space=pltpu.VMEM)


def peer(index, step, count):
    if count & (count - 1) == 0:
        return index ^ step
    return (index + step) % count


def split(x):
    high = x.astype(BF16)
    return high, (x - high.astype(F32)).astype(BF16)


def dot(a, b):
    return jnp.dot(a, b, preferred_element_type=F32)


def dot_nt(a, b):
    return lax.dot_general(a, b, (((1,), (1,)), ((), ())), preferred_element_type=F32)


def dot_three(a_high, a_low, b):
    b_high, b_low = split(b)
    return dot(a_high, b_high) + (dot(a_high, b_low) + dot(a_low, b_high))


def dot_exact(a, b):
    return jnp.dot(a, b, preferred_element_type=F32, precision=HIGH)


def struct(shape, dtype=F32):
    return pltpu.VMEM(shape, dtype)


def local(*arrays):
    return [pltpu.with_memory_space_constraint(a, pltpu.VMEM) for a in arrays]


def params(nbytes=0):
    return pltpu.CompilerParams(vmem_limit_bytes=16 * 2**20 + 2 * nbytes)


def cost(flops, nbytes):
    return pl.CostEstimate(flops=flops, bytes_accessed=nbytes, transcendentals=0)


def write_faces(layers, u, a_i, b_i, a_j, b_j):
    odd_s = lax.rem(lax.axis_index("surf"), 2)
    odd_c = lax.rem(lax.axis_index("col"), 2)
    rows_a = pl.multiple_of((1 - odd_s) * (NODES - FACE), FACE)
    rows_b = pl.multiple_of(odd_s * (NODES - FACE), FACE)
    j_a = (1 - odd_c) * (FACE - EDGE)
    j_b = odd_c * (FACE - EDGE)
    for d in range(layers):
        a_i[d] = u[d, pl.ds(rows_a, FACE), :]
        b_i[d] = u[d, pl.ds(rows_b, FACE), :]
        for i in range(EDGE):
            to = pl.ds(i * EDGE, EDGE)
            a_j[d, to, :] = u[d, pl.ds(pl.multiple_of(i * FACE + j_a, EDGE), EDGE), :]
            b_j[d, to, :] = u[d, pl.ds(pl.multiple_of(i * FACE + j_b, EDGE), EDGE), :]


def layer_of(value, k):
    return value.reshape(FACE, EDGE, value.shape[-1])[:, k, :]


def put_layer(base, value, k):
    fields = base.shape[-1]
    height = lax.broadcasted_iota(jnp.int32, (FACE, EDGE, fields), 1)
    wide = jnp.broadcast_to(value[:, None, :], (FACE, EDGE, fields))
    return base + jnp.where(height == k, wide, 0.0).reshape(NODES, fields)


def top_kernel(u, top, held, sem):
    copy = pltpu.make_async_copy(u.at[0], held, sem)
    copy.start()
    copy.wait()
    top[...] = layer_of(held[...], 0)


def top_of(u):
    _, nodes, fields = u.shape
    return pl.pallas_call(
        top_kernel,
        out_shape=struct((FACE, fields)),
        in_specs=[pl.BlockSpec(memory_space=pl.ANY)],
        out_specs=VMEM,
        scratch_shapes=[pltpu.VMEM((nodes, fields), F32), pltpu.SemaphoreType.DMA],
        compiler_params=params(),
        name="top_of",
    )(u)


def faces_kernel(layers, u, after, *faces):
    write_faces(layers, u, *faces)


def faces_of(u, after):
    layers, _, fields = u.shape
    return pl.pallas_call(
        functools.partial(faces_kernel, layers),
        out_shape=[struct((layers, FACE, fields))] * 4,
        in_specs=[VMEM] * 2,
        out_specs=[VMEM] * 4,
        compiler_params=params(),
        name="faces_of",
    )(*local(u, after))


def update_kernel(layers, w, top, a_i, b_i, a_j, b_j, u, *faces):
    u[...] = w[...]
    add_neighbours(layers, u, a_i, b_i, a_j, b_j)
    base = u[0]
    height = lax.rem(lax.broadcasted_iota(jnp.int32, base.shape, 0), EDGE)
    u[0] = put_layer(jnp.where(height == 0, 0.0, base), top[...], 0)
    write_faces(layers, u, *faces)


def update(w, top, faces):
    layers, _, fields = w.shape
    face = struct((layers, FACE, fields))
    return pl.pallas_call(
        functools.partial(update_kernel, layers),
        out_shape=[struct(w.shape)] + [face] * 4,
        in_specs=[VMEM] * 6,
        out_specs=[VMEM] * 5,
        compiler_params=params(),
        name="update",
    )(*local(w, top, *faces))


def swap_faces(faces):
    out = []
    for axis, (first, second) in zip(("surf", "col"), (faces[:2], faces[2:])):
        count = lax.axis_size(axis)
        pairs_a = [(i, i ^ 1) for i in range(count) if i ^ 1 < count]
        pairs_b = [(i, ((i + 1) ^ 1) - 1) for i in range(1, count) if ((i + 1) ^ 1) - 1 < count]
        out.append(lax.ppermute(first, axis, pairs_a))
        out.append(lax.ppermute(second, axis, pairs_b))
    return out


def tables_kernel(cols, per_pair, count, bem, m, nh, nl, ch, cl, own, xt, yt, ah, al):
    group = bem.shape[1]
    s = lax.axis_index("surf")
    c = lax.axis_index("col")
    step = pl.program_id(0)
    nodes_all = jnp.broadcast_to(bem[...], (FACE, group))
    lane = lax.broadcasted_iota(jnp.int32, (FACE, group), 1)
    index = lax.broadcasted_iota(jnp.int32, (FACE, group), 0)
    mine = index + s * FACE
    hit_node = nodes_all == mine

    @pl.when(step == 0)
    def _():
        for k in range(cols):
            high, low = split(m[peer(c, k, cols)])
            ah[pl.ds(k * FACE, FACE), :] = high
            al[pl.ds(k * FACE, FACE), :] = low
        r = lax.broadcasted_iota(jnp.int32, (FACE, FACE), 0)
        l = lax.broadcasted_iota(jnp.int32, (FACE, FACE), 1)

        def column(mask, value):
            return jnp.sum(jnp.where(mask, value, 0.0), axis=1, keepdims=True)

        def row(mask, value):
            return dot_nt(value.astype(BF16), jnp.where(mask, 1.0, 0.0).astype(BF16))

        block_of = (lane // FACE).astype(F32)
        hold_c, hold_r = column(hit_node, block_of), row(hit_node, block_of)
        same = (hold_c == hold_r) & (l < r)
        rank_c = jnp.sum(jnp.where(same, 1.0, 0.0), axis=1, keepdims=True)
        place_c = (hold_c * per_pair + rank_c).astype(jnp.int32)
        xt[...] = jnp.where(l == place_c, 1.0, 0.0)

        hit = lane == mine
        owner = (nodes_all // FACE).astype(F32)
        local = lax.rem(nodes_all, FACE).astype(F32)
        own_c, own_r = column(hit, owner), row(hit, owner)
        loc_c, loc_r = column(hit, local), row(hit, local)
        same = (own_c == own_r) & (loc_c < loc_r)
        rank_r = jnp.sum(jnp.where(same, 1.0, 0.0), axis=0, keepdims=True)
        place_r = (own_r * per_pair + rank_r).astype(jnp.int32)
        yt[...] = jnp.where(r == place_r, 1.0, 0.0)

    ones_own = jnp.where(hit_node, 1.0, 0.0).astype(BF16)
    high, low = ah[...], al[...]
    for q in range(count):
        block = (s ^ (step * count + q)) * FACE
        by_slot = jnp.where(lane == index + block, -damping, 0.0).astype(BF16)
        by_node = jnp.where(nodes_all == index + block, 1.0, 0.0).astype(BF16)
        pick = jnp.concatenate([by_slot, by_node], axis=0)
        here = pl.ds(q * 2 * FACE, 2 * FACE)
        picked_high = dot_nt(high, pick).astype(BF16)
        picked_low = dot_nt(low, pick).astype(BF16)
        ch[:, here] = picked_high
        cl[:, here] = picked_low
        nh[:, pl.ds(q * FACE, FACE)] = picked_high[:, FACE:]
        nl[:, pl.ds(q * FACE, FACE)] = picked_low[:, FACE:]
        own[:, here] = dot_nt(ones_own, pick).astype(BF16)


def tables(bem, m, per_pair):
    cols, _, group = m.shape
    rows = cols * FACE
    surfs = group // FACE
    count = min(surfs, EDGE)
    fixed = lambda shape: pl.BlockSpec(shape, lambda i: (0,) * len(shape))
    wide = lambda height, width: pl.BlockSpec((height, width), lambda i: (0, i))
    return pl.pallas_call(
        functools.partial(tables_kernel, cols, per_pair, count),
        grid=(surfs // count,),
        out_shape=[struct((rows, group), BF16)] * 2
        + [struct((rows, 2 * group), BF16)] * 2
        + [struct((FACE, 2 * group), BF16)]
        + [struct((FACE, FACE))] * 2,
        in_specs=[fixed((1, group)), fixed(m.shape)],
        out_specs=[wide(rows, count * FACE)] * 2
        + [wide(rows, 2 * count * FACE)] * 2
        + [wide(FACE, 2 * count * FACE)]
        + [fixed((FACE, FACE))] * 2,
        scratch_shapes=[pltpu.VMEM((rows, group), BF16)] * 2,
        cost_estimate=cost(8 * rows * group * group, 10 * rows * group),
        compiler_params=params(4 * m.size),
        name="tables",
    )(bem, m)


def edge_rows(top, high):
    fields = top.shape[-1]
    columns = top.reshape(EDGE, EDGE, fields)
    return jnp.where(high, columns[:, EDGE - 1, :], columns[:, 0, :])


def operator_kernel(cols, blocks, select, mh, ml, extra, *refs):
    s = lax.axis_index("surf")
    c = lax.axis_index("col")
    if len(blocks) == 1:
        trace = [refs[0][s ^ p] for p in range(blocks[0])]
    else:
        trace = [ref[...] for ref in refs[: len(blocks)]]
    outs = refs[len(blocks) :]
    value = jnp.concatenate(trace, axis=0)
    high, low = split(value)
    part = dot(mh[...], high) + (dot(mh[...], low) + dot(ml[...], high))
    for k in range(cols):
        outs[k][pl.ds(0, FACE), :] = part[k * FACE : (k + 1) * FACE]
    if select:
        rest = (value - high.astype(F32) - low.astype(F32)).astype(BF16)
        pick = extra[...]
        outs[cols][...] = dot(pick, high) + (dot(pick, low) + dot(pick, rest))
    else:
        odd = lax.rem(c, 2) == 1
        for k, high_edge in edge_steps(cols, odd):
            outs[k][pl.ds(FACE, EDGE), :] = edge_rows(trace[0], high_edge)


def edge_steps(cols, odd):
    steps = []
    if cols > 1:
        steps.append((1, jnp.logical_not(odd)))
    if cols > 2:
        steps.append((cols - 1, odd))
    return steps


def operator(cols, mh, ml, trace, extra, select):
    trace = trace if isinstance(trace, list) else [trace]
    fields = trace[0].shape[-1]
    heights = [FACE] * (cols + select)
    if not select:
        for k, _ in edge_steps(cols, False):
            heights[k] += EDGE
    args = (mh, ml, extra) + tuple(trace)
    return pl.pallas_call(
        functools.partial(operator_kernel, cols, [t.shape[0] for t in trace], select),
        out_shape=[struct((h, fields)) for h in heights],
        in_specs=[VMEM] * len(args),
        out_specs=[VMEM] * len(heights),
        cost_estimate=cost(6 * mh.size * fields, 4 * mh.size + 4 * mh.shape[1] * fields),
        compiler_params=params(4 * mh.size),
        name="operator",
    )(*local(*args))


def gather_blocks(x, axis):
    count = lax.axis_size(axis)
    if count & (count - 1) or count > MAX_PERMUTES:
        return exchange(jnp.broadcast_to(x[None], (count,) + x.shape))

    def send(block, step):
        return lax.ppermute(block, axis, [(i, i ^ step) for i in range(count)])

    half = count // 2
    far = send(x, half)
    steps = [*range(2, half), 1]
    near = {step: send(x, step) for step in steps}
    passed = {step + half: send(far, step) for step in steps}
    found = {0: x, half: far, **near, **passed}
    return [found[step] for step in range(count)]


def reduce_rows(parts):
    count = len(parts)
    got = [
        lax.ppermute(parts[k], "col", [(i, peer(i, k, count)) for i in range(count)])
        for k in range(1, count)
    ]
    return [parts[0]] + got


def shifted(top, low, high, axis):
    fields = top.shape[-1]
    empty = jnp.zeros_like(top).reshape(EDGE, EDGE, fields)
    place = lax.broadcasted_iota(jnp.int32, empty.shape, axis)
    low, high = (jnp.expand_dims(edge, axis) for edge in (low, high))
    return (jnp.where(place == 0, low, 0.0) + jnp.where(place == EDGE - 1, high, 0.0)).reshape(top.shape)


def traction_kernel(cols, surfs, blocks, *refs):
    s, c = lax.axis_index("surf"), lax.axis_index("col")
    parts, refs = refs[:cols], refs[cols:]
    top, tops, out = refs[0], refs[1:-1], refs[-1]
    body = pl.ds(0, FACE)
    out[body, :] = sum(p[body, :] for p in parts[1:]) + parts[0][body, :]

    def block(position, rows):
        if len(tops) == 1:
            return tops[0][jnp.clip(position, 0, surfs - 1), rows, :]
        found, step = jnp.zeros((EDGE, top.shape[1]), F32), 1
        while step < surfs:
            found = jnp.where(position == s ^ step, tops[step][rows, :], found)
            step = 2 * step + 1
        return found

    value = top[...]
    low = jnp.where(s > 0, block(s - 1, pl.ds(FACE - EDGE, EDGE)), 0.0)
    high = jnp.where(s < surfs - 1, block(s + 1, pl.ds(0, EDGE)), 0.0)
    near = shifted(value, low, high, 0)
    odd = lax.rem(c, 2) == 1
    low, high = (jnp.zeros((EDGE, top.shape[1]), F32) for _ in range(2))
    for k, is_high in edge_steps(cols, odd):
        edge = parts[k][pl.ds(FACE, EDGE), :]
        low = jnp.where(jnp.logical_not(is_high) & (c > 0), edge, low)
        high = jnp.where(is_high & (c < cols - 1), edge, high)
    near = near + shifted(value, low, high, 1)
    out[pl.ds(FACE, FACE), :] = value + damping * coupling * near


def traction_and_top(parts, top, tops, surfs):
    tops = tops if isinstance(tops, list) else [tops]
    args = (*parts, top, *tops)
    return pl.pallas_call(
        functools.partial(traction_kernel, len(parts), surfs, len(tops)),
        out_shape=struct((2 * FACE, top.shape[1])),
        in_specs=[VMEM] * len(args),
        out_specs=VMEM,
        compiler_params=params(),
        name="traction_and_top",
    )(*local(*args))


def last_traction_kernel(count, *refs):
    parts, (yt, after, total_ref, sorted_ref) = refs[:count], refs[count:]
    total = sum(p[...] for p in parts[1:]) + parts[0][...]
    total_ref[...] = total
    sorted_ref[...] = dot_exact(yt[...], total)


def last_traction(parts, yt, after):
    return pl.pallas_call(
        functools.partial(last_traction_kernel, len(parts)),
        out_shape=[jax.ShapeDtypeStruct(parts[0].shape, F32), struct(parts[0].shape)],
        in_specs=[VMEM] * (len(parts) + 2),
        out_specs=[VMEM] * 2,
        compiler_params=params(),
        name="last_traction",
    )(*local(*parts, yt, after))


def volume_kernel(layers, k, load, u, out, top):
    half = damping * coupling
    fields = u.shape[-1]
    height = lax.rem(lax.broadcasted_iota(jnp.int32, (NODES, fields), 0), EDGE)
    for d in range(layers):
        here = u[d]
        k_high, k_low = split(k[d])
        applied = dot_three(k_high, k_low, here)
        deeper = here
        if d + 1 < layers:
            deeper = here - pltpu.roll(u[d + 1], EDGE - 1, 0)
        vertical = jnp.where(height == EDGE - 1, deeper, 0.0)
        if d > 0:
            above = here - pltpu.roll(u[d - 1], NODES - EDGE + 1, 0)
            vertical = jnp.where(height == 0, above, vertical)
        out[d] = here + damping * (load[d] - applied) - half * vertical

        def own_face(rows):
            out[d, rows, :] = out[d, rows, :] - half * u[d, rows, :]

        own_face(pl.ds(0, FACE))
        own_face(pl.ds(NODES - FACE, FACE))
        for i in range(EDGE):
            own_face(pl.ds(i * FACE, EDGE))
            own_face(pl.ds(i * FACE + FACE - EDGE, EDGE))
    top[...] = layer_of(out[0], 0)


def volume(kmats, load, u):
    layers, nodes, fields = u.shape
    return pl.pallas_call(
        functools.partial(volume_kernel, layers),
        out_shape=[struct(u.shape), struct((FACE, fields))],
        in_specs=[VMEM] * 3,
        out_specs=[VMEM] * 2,
        cost_estimate=cost(6 * layers * nodes * nodes * fields, 4 * layers * nodes * (nodes + 3 * fields)),
        compiler_params=params(),
        name="volume",
    )(*local(kmats, load, u))


def add_neighbours(layers, out, a_i, b_i, a_j, b_j):
    odd_s = lax.rem(lax.axis_index("surf"), 2) == 1
    odd_c = lax.rem(lax.axis_index("col"), 2) == 1
    half = damping * coupling

    def face(d, rows, first, second, odd):
        out[d, rows, :] = out[d, rows, :] + half * jnp.where(odd, first, second)

    for d in range(layers):
        got_a, got_b = a_i[d], b_i[d]
        face(d, pl.ds(0, FACE), got_a, got_b, odd_s)
        face(d, pl.ds(NODES - FACE, FACE), got_b, got_a, odd_s)
        for i in range(EDGE):
            rows = pl.ds(i * EDGE, EDGE)
            got_a, got_b = a_j[d, rows, :], b_j[d, rows, :]
            face(d, pl.ds(i * FACE, EDGE), got_a, got_b, odd_c)
            face(d, pl.ds(i * FACE + FACE - EDGE, EDGE), got_b, got_a, odd_c)


def neighbours_kernel(layers, w, a_i, b_i, a_j, b_j, out, first):
    out[...] = w[...]
    add_neighbours(layers, out, a_i, b_i, a_j, b_j)
    first[...] = out[0]


def neighbours(w, faces):
    _, nodes, fields = w.shape
    return pl.pallas_call(
        functools.partial(neighbours_kernel, w.shape[0]),
        out_shape=[jax.ShapeDtypeStruct(w.shape, F32), struct((nodes, fields))],
        in_specs=[VMEM] * 5,
        out_specs=[VMEM] * 2,
        compiler_params=params(),
        name="neighbours",
    )(*local(w, *faces))


def finish_kernel(all_ref, first, xt, got, out, held, sem):
    held[...] = put_layer(first[...], -damping * dot_exact(xt[...], got[...]), 0)
    copy = pltpu.make_async_copy(held, out.at[0], sem)
    copy.start()
    copy.wait()


def finish(whole, first, xt, got):
    anywhere = pl.BlockSpec(memory_space=pl.ANY)
    return pl.pallas_call(
        finish_kernel,
        out_shape=jax.ShapeDtypeStruct(whole.shape, F32),
        in_specs=[anywhere] + [VMEM] * 3,
        out_specs=anywhere,
        scratch_shapes=[pltpu.VMEM(first.shape, F32), pltpu.SemaphoreType.DMA],
        input_output_aliases={0: 0},
        compiler_params=params(),
        name="finish",
    )(whole, *local(first, xt, got))


def exchange(blocks):
    return lax.all_to_all(blocks, "surf", split_axis=0, concat_axis=0, tiled=True)


def shards(stiffness, load, start, boundary_matrix, bem_node):
    surfs, cols = lax.axis_size("surf"), lax.axis_size("col")
    per_pair = max(FACE // surfs, 1)
    kmats, load, u = stiffness[0], load[0], start[0]
    fields = load.shape[2]
    tops = gather_blocks(top_of(u), "surf")
    nh, nl, ch, cl, own, xt, yt = tables(
        bem_node, jnp.transpose(boundary_matrix, (1, 0, 2)), per_pair
    )
    w, top = volume(kmats, load, u)
    parts = operator(cols, nh, nl, tops, top, False)
    faces = faces_of(u, parts[0])
    parts = reduce_rows(parts)
    pair = traction_and_top(parts, top, tops, surfs)
    faces = swap_faces(faces)
    *parts, top = operator(cols, ch, cl, gather_blocks(pair, "surf"), own, True)
    parts = reduce_rows(parts)
    u, *faces = update(w, top, faces)
    faces = swap_faces(faces)
    w, top = volume(kmats, load, u)
    traction, back = last_traction(parts, yt, top)
    back = exchange(back.reshape(surfs, per_pair, fields)).reshape(FACE, fields)
    return finish(*neighbours(w, faces), xt, back)[None], traction[None]


def solution(mesh):
    cell = P(("surf", "col"), None, None, None)
    return jax.shard_map(
        shards,
        mesh=mesh,
        in_specs=(cell, cell, cell, P("surf", None, "col"), P("col", None)),
        out_specs=(cell, P("col", "surf", None)),
        check_vma=False,
    )
```
